32 devices in a mesh: depth: 2 (over x), map: 16 (over z, y, core).
Axes of the slice: x: 2, y: 2, z: 4, core: 2. Of those that a mesh axis runs over, the one named last changes fastest.
Arguments:
- velocity: float32 [3, 32, 512, 128], P(None, 'depth', 'map'), may hold values from -6 to 6
- stress: float32 [6, 32, 512, 128], P(None, 'depth', 'map'), may hold values from -6 to 6
- region: int32 [32, 512, 128], P('depth', 'map'), may hold values from 0 to 7
- lame_table: float32 [8], replicated, may hold values from 0.2 to 0.5
- shear_table: float32 [8], replicated, may hold values from 0.1 to 0.3
- buoyancy_table: float32 [8], replicated, may hold values from 0.6 to 1.2
- height: float32 [256, 4096], P('depth', 'map'), may hold values from -6 to 6
- discharge: float32 [2, 256, 4096], P(None, 'depth', 'map'), may hold values from -6 to 6
- face_depth: float32 [2, 256, 4096], P(None, 'depth', 'map'), may hold values from 0.5 to 2
- wet: int32 [256, 4096], P('depth', 'map'), may hold values 0 or 1
- seafloor_index: int32 [256, 4096], P('depth', 'map'), may hold values from 0 to 4095
Outputs:
- velocity_out: float32 [3, 32, 512, 128], P(None, 'depth', 'map')
- stress_out: float32 [6, 32, 512, 128], P(None, 'depth', 'map')
- height_out: float32 [256, 4096], P('depth', 'map')
- discharge_out: float32 [2, 256, 4096], P(None, 'depth', 'map')
The draws below stay inside these ranges and needn't reach their ends.
Inputs may be any that keep to these rules, and one draw needn't show every extreme that they name: `wet`: 1 for a wet ocean cell, 0 for a dry one. `seafloor_index`: index k of the seafloor cell under an ocean cell, among the 32 x 128 crust cells of its own map column, counted row by row.
All inputs are finite; a program needn't handle non-finite values. No bound on the sum of `wet` on one device may be relied on, other than what follows from the above.
Results may differ from the reference program's by a relative error of at most 0.000054.
Values sent between devices are 32-bit elements; how exact they have to be, the bound alone decides.
No kernel may reach another device: no remote copies, remote signals or barrier semaphores. Data moves between devices by JAX's collectives and lax.ppermute only.
A program may use at most 64 MiB of HBM per device.

```python
import math
import jax
import jax.numpy as jnp
from jax import lax

CX = 32
NY = 128
REGIONS = 8
ITERS = 3
OC = 256
OSTEPS = 2
NZ = 32
NX = 512
NOR = 256
NOC = 4096


def plant(drawn, stream_key, least, high):
    index_at = [jax.random.randint(jax.random.fold_in(stream_key, axis), (), 0, length) for axis, length in enumerate(drawn.shape)]
    widest = drawn.shape.index(max(drawn.shape))
    beside = index_at[:widest] + [(index_at[widest] + 1) % drawn.shape[widest]] + index_at[widest + 1:]
    return drawn.at[tuple(index_at)].set(least).at[tuple(beside)].set(high)


def levels(stream_key, shape, pieces, least, largest):
    gain, own = 1.0, jax.random.fold_in(stream_key, 6)
    for dim, blocks in pieces:
        steps = jnp.exp(jax.random.uniform(jax.random.fold_in(own, dim), (blocks,), jnp.float32, least / len(pieces), largest / len(pieces)))
        gain = gain * jnp.repeat(steps, shape[dim] // blocks).reshape([-1 if axis == dim else 1 for axis in range(len(shape))])
    return gain


def bell_draw(stream_key, shape, scale, reach, shards=(), kind=jnp.bfloat16):
    factor_of = levels(stream_key, shape, shards, -0.22, 0.18) if shards else 1.0
    array = jax.random.normal(stream_key, shape, jnp.float32) * scale * factor_of
    return jnp.minimum(jnp.maximum(array, -reach), reach).astype(kind)


def setup_inputs(seed: int = 0) -> dict:
    seeds = jax.random.split(jax.random.key(seed), 12)
    return {
        "velocity": bell_draw(seeds[0], (3, NZ, NX, NY), 1.0, 6.0, ((1, 2), (2, 16)), jnp.float32),
        "stress": bell_draw(seeds[1], (6, NZ, NX, NY), 1.0, 6.0, ((1, 2), (2, 16)), jnp.float32),
        "region": plant(jax.random.randint(seeds[2], (NZ, NX, NY), 0, REGIONS), jax.random.fold_in(seeds[2], 1), 0, REGIONS - 1).astype(jnp.int32),
        "lame_table": jnp.clip(jax.random.uniform(seeds[3], (REGIONS,), jnp.float32, 0.2, 0.5), 0.2, 0.5),
        "shear_table": jnp.clip(jax.random.uniform(seeds[4], (REGIONS,), jnp.float32, 0.1, 0.3), 0.1, 0.3),
        "buoyancy_table": jnp.clip(jax.random.uniform(seeds[5], (REGIONS,), jnp.float32, 0.6, 1.2), 0.6, 1.2),
        "height": bell_draw(seeds[6], (NOR, NOC), 1.0, 6.0, ((0, 2), (1, 16)), jnp.float32),
        "discharge": bell_draw(seeds[7], (2, NOR, NOC), 1.0, 6.0, ((1, 2), (2, 16)), jnp.float32),
        "face_depth": jnp.clip(jnp.exp(math.log(2.0) - 1.3862944 * jax.random.uniform(seeds[8], (2, NOR, NOC), jnp.float32) ** levels(seeds[8], (2, NOR, NOC), ((1, 2), (2, 16)), -0.2, 0.2)), 0.5, 2.0),
        "wet": plant((jax.random.randint(seeds[9], (NOR, NOC), 0, 4) < 3).astype(jnp.int32), jax.random.fold_in(seeds[9], 1), 0, 1),
        "seafloor_index": plant(jax.random.randint(seeds[10], (NOR, NOC), 0, CX * NY), jax.random.fold_in(seeds[10], 1), 0, (CX * NY) - 1).astype(jnp.int32),
    }


near_coef = 9.0 / 8.0
far_coef = 1.0 / 24.0
time_step = 0.2
ocean_step = 0.2
gravity = 1.0


def cells(padded, axis, offset, count):
    return lax.slice_in_dim(padded, offset, offset + count, axis=axis)


def forward_diff(padded, axis):
    count = padded.shape[axis] - 4
    return near_coef * (cells(padded, axis, 3, count) - cells(padded, axis, 2, count)) - far_coef * (cells(padded, axis, 4, count) - cells(padded, axis, 1, count))


def backward_diff(padded, axis):
    count = padded.shape[axis] - 4
    return near_coef * (cells(padded, axis, 2, count) - cells(padded, axis, 1, count)) - far_coef * (cells(padded, axis, 3, count) - cells(padded, axis, 0, count))


def forward_y(field):
    return near_coef * (jnp.roll(field, -1, 2) - field) - far_coef * (jnp.roll(field, -2, 2) - jnp.roll(field, 1, 2))


def backward_y(field):
    return near_coef * (field - jnp.roll(field, 1, 2)) - far_coef * (jnp.roll(field, -1, 2) - jnp.roll(field, 2, 2))


def pad_map(field):
    return jnp.pad(field, ((0, 0), (2, 2), (0, 0)))


def pad_depth(field):
    return jnp.pad(field, ((2, 2), (0, 0), (0, 0)))


def reference(velocity, stress, region, lame_table, shear_table, buoyancy_table, height, discharge, face_depth, wet, seafloor_index):
    lame = jnp.take(lame_table, region)
    shear = jnp.take(shear_table, region)
    buoyancy = jnp.take(buoyancy_table, region)
    speeds = [velocity[0], velocity[1], velocity[2]]
    forces = [stress[index] for index in range(6)]
    lift = jnp.zeros((velocity.shape[2], velocity.shape[3]), jnp.float32)
    for turn in range(ITERS):
        speed_x = speeds[0] + time_step * buoyancy * (forward_diff(pad_map(forces[0]), 1) + backward_y(forces[1]) + backward_diff(pad_depth(forces[2]), 0))
        speed_y = speeds[1] + time_step * buoyancy * (backward_diff(pad_map(forces[1]), 1) + forward_y(forces[5]) + backward_diff(pad_depth(forces[3]), 0))
        speed_z = speeds[2] + time_step * buoyancy * (backward_diff(pad_map(forces[2]), 1) + backward_y(forces[3]) + forward_diff(pad_depth(forces[4]), 0))
        speeds = [speed_x, speed_y, speed_z]
        lift = lift + time_step * speed_z[0]
        strain_x = backward_diff(pad_map(speed_x), 1)
        strain_y = backward_y(speed_y)
        strain_z = backward_diff(pad_depth(speed_z), 0)
        spread = strain_x + strain_y + strain_z
        forces = [
            forces[0] + time_step * (lame * spread + 2.0 * shear * strain_x),
            forces[1] + time_step * shear * (forward_y(speed_x) + forward_diff(pad_map(speed_y), 1)),
            forces[2] + time_step * shear * (forward_diff(pad_depth(speed_x), 0) + forward_diff(pad_map(speed_z), 1)),
            forces[3] + time_step * shear * (forward_diff(pad_depth(speed_y), 0) + forward_y(speed_z)),
            forces[4] + time_step * (lame * spread + 2.0 * shear * strain_z),
            forces[5] + time_step * (lame * spread + 2.0 * shear * strain_y),
        ]
    rate = speeds[2][0]
    tile_size = CX * NY
    column = (jnp.arange(NOC, dtype=jnp.int32) // OC) * tile_size
    where = seafloor_index + column[None, :]
    lift_at = jnp.take(lift.reshape(-1), where)
    rate_at = jnp.take(rate.reshape(-1), where)
    wetness = wet.astype(jnp.float32)
    level = wetness * (height + lift_at)
    source = wetness * rate_at
    zero_col = jnp.zeros((NOR, 1), jnp.float32)
    zero_row = jnp.zeros((1, NOC), jnp.float32)
    wet_east = jnp.concatenate([wetness[:, 1:], zero_col], axis=1)
    wet_north = jnp.concatenate([wetness[1:, :], zero_row], axis=0)
    mask_x = wetness * wet_east
    mask_y = wetness * wet_north
    depth_x = face_depth[0] * mask_x
    depth_y = face_depth[1] * mask_y
    flux_x = discharge[0] * mask_x
    flux_y = discharge[1] * mask_y
    for turn in range(OSTEPS):
        level_east = jnp.concatenate([level[:, 1:], zero_col], axis=1)
        level_north = jnp.concatenate([level[1:, :], zero_row], axis=0)
        flux_x = flux_x - ocean_step * gravity * depth_x * (level_east - level)
        flux_y = flux_y - ocean_step * gravity * depth_y * (level_north - level)
        flux_west = jnp.concatenate([zero_col, flux_x[:, :-1]], axis=1)
        flux_south = jnp.concatenate([zero_row, flux_y[:-1, :]], axis=0)
        level = level - ocean_step * wetness * ((flux_x - flux_west) + (flux_y - flux_south)) + ocean_step * source
    return jnp.stack(speeds), jnp.stack(forces), level, jnp.stack([flux_x, flux_y])
```

```python
import functools

import jax
import jax.numpy as jnp
from jax import lax
from jax.experimental import pallas as pl
from jax.experimental.pallas import tpu as pltpu
from jax.sharding import PartitionSpec as P

ITERS = 3
OSTEPS = 2
LANES = 128
PAD = 8

near_coef = 9.0 / 8.0
far_coef = 1.0 / 24.0
time_step = 0.2
ocean_step = 0.2
gravity = 1.0

VMEM = pl.BlockSpec(memory_space=pltpu.VMEM)
SMEM = pl.BlockSpec(memory_space=pltpu.SMEM)
ANY = pl.BlockSpec(memory_space=pl.ANY)
F32 = jnp.float32

BACK = (2, 1)
FORTH = (1, 2)
STRESS_MAP = ((0, FORTH), (1, BACK), (2, BACK))
STRESS_DEPTH = ((2, BACK), (3, BACK), (4, FORTH))
SPEED_MAP = ((0, BACK), (1, FORTH), (2, FORTH))
SPEED_DEPTH = ((0, FORTH), (1, FORTH), (2, BACK))
SLOTS = 5


def slots(spec, side):
    found = {}
    for field, need in spec:
        cells = range(-need[0], 0) if side == 0 else range(need[1])
        for cell in cells:
            found[(field, cell)] = len(found)
    return found


def swap_pairs(count):
    first = [(i, i ^ 1) for i in range(count) if i ^ 1 < count]
    second = [(i, i + 1) for i in range(1, count - 1, 2)]
    return first, sorted(second + [(j, i) for i, j in second])


def swap(x, axis, phase):
    return lax.ppermute(x, axis, swap_pairs(lax.axis_size(axis))[phase])


def even(axis):
    return lax.rem(lax.axis_index(axis), 2) == 0


def roll(x, by):
    return pltpu.roll(x, by % x.shape[1], 1)


def diff_forward(at):
    return near_coef * (at(1) - at(0)) - far_coef * (at(2) - at(-1))


def diff_backward(at):
    return near_coef * (at(0) - at(-1)) - far_coef * (at(1) - at(-2))


def forward_y(x):
    return near_coef * (roll(x, -1) - x) - far_coef * (roll(x, -2) - roll(x, 1))


def backward_y(x):
    return near_coef * (x - roll(x, 1)) - far_coef * (roll(x, -1) - roll(x, 2))


def emit(spec, cell, size, parity_even, outs, store):
    def fill(out, side):
        for (field, offset), slot in slots(spec, side).items():
            store(out, slot, cell(field, size + offset if side == 0 else offset))

    @pl.when(parity_even)
    def _():
        fill(outs[0], 0)
        if len(outs) > 1:
            fill(outs[1], 1)

    @pl.when(jnp.logical_not(parity_even))
    def _():
        fill(outs[0], 1)
        if len(outs) > 1:
            fill(outs[1], 0)


def store_slot(out, slot, value):
    out[slot] = value


def emit_all(map_spec, depth_spec, read, layers, columns, depth_outs, map_outs):
    emit(depth_spec, lambda f, i: read(f, i, None), layers, even("depth"), depth_outs, store_slot)
    emit(map_spec, lambda f, i: read(f, None, i), columns, even("map"), map_outs, store_slot)


def edge_kernel(n_depth, ocean_n, layers, columns, stress, *refs):
    ocean = refs[:ocean_n]
    refs = refs[ocean_n:]
    depth_outs, map_outs = refs[:n_depth], refs[n_depth : n_depth + 2]
    low_c, high_c, low_d, high_d, low_o, high_o, sem = refs[n_depth + 2 :]
    copies = [
        (stress.at[pl.ds(0, 3), :, pl.ds(0, PAD)], low_c),
        (stress.at[pl.ds(0, 3), :, pl.ds(columns - PAD, PAD)], high_c),
        (stress.at[pl.ds(2, 3), pl.ds(0, 2)], low_d),
        (stress.at[pl.ds(2, 3), pl.ds(layers - 2, 2)], high_d),
    ]
    rows = ocean[0].shape[-2]
    for i, ref in enumerate(ocean):
        copies.append((ref.at[pl.ds(0, PAD)], low_o.at[i]))
        copies.append((ref.at[pl.ds(rows - PAD, PAD)], high_o.at[i]))
    copies = [pltpu.make_async_copy(a, b, sem.at[i]) for i, (a, b) in enumerate(copies)]
    for copy in copies:
        copy.start()
    for copy in copies:
        copy.wait()

    def read(field, layer, column):
        if column is None:
            return low_d[field - 2, layer] if layer < 2 else high_d[field - 2, layer - (layers - 2)]
        if column < PAD:
            return low_c[field, :, column]
        return high_c[field, :, column - (columns - PAD)]

    emit_all(STRESS_MAP, STRESS_DEPTH, read, layers, columns, depth_outs, map_outs)
    tiles = low_o.shape[2] // LANES

    def rows_out(out, side):
        source, first = (high_o, PAD - 2) if side == 0 else (low_o, 0)
        for i in range(ocean_n):
            for k in range(2):
                for t in range(tiles):
                    line = (i * 2 + k) * tiles + t
                    part = source[i, pl.ds(first + k, 1), pl.ds(t * LANES, LANES)]
                    out[SLOTS, pl.ds(line, 1), :] = part

    @pl.when(even("depth"))
    def _():
        rows_out(depth_outs[0], 0)
        if n_depth > 1:
            rows_out(depth_outs[1], 1)

    @pl.when(jnp.logical_not(even("depth")))
    def _():
        rows_out(depth_outs[0], 1)
        if n_depth > 1:
            rows_out(depth_outs[1], 0)


def material_kernel(lame_t, shear_t, buoy_t, region, dtb, dtl, dts):
    def body(p, _):
        r = region[p]
        b = jnp.full(r.shape, time_step * buoy_t[0], F32)
        l = jnp.full(r.shape, time_step * lame_t[0], F32)
        s = jnp.full(r.shape, time_step * shear_t[0], F32)
        for value in range(1, buoy_t.shape[0]):
            here = r == value
            b = jnp.where(here, time_step * buoy_t[value], b)
            l = jnp.where(here, time_step * lame_t[value], l)
            s = jnp.where(here, time_step * shear_t[value], s)
        dtb[p] = b
        dtl[p] = l
        dts[p] = s
        return 0

    lax.fori_loop(0, region.shape[0], body, 0)


def take_halos(spec, axis, received, below, above):
    zero = jnp.zeros(below.shape, F32)

    def halo(i):
        return received[i][0:SLOTS] if i < len(received) else zero

    @pl.when(even(axis))
    def _():
        above[...] = halo(0)
        below[...] = halo(1)

    @pl.when(jnp.logical_not(even(axis)))
    def _():
        below[...] = halo(0)
        above[...] = halo(1)


def build_map(spec, source, wide, received, layers, columns):
    def body(p, _):
        for field, _need in spec:
            wide[field, p, pl.ds(PAD, columns)] = source[field, p]
        return 0

    lax.fori_loop(0, layers, body, 0, unroll=4)

    def put(ref, side):
        for (field, offset), slot in slots(spec, side).items():
            at = PAD + offset if side == 0 else PAD + columns + offset
            wide[field, :, at] = ref[slot]

    @pl.when(even("map"))
    def _():
        put(received[0], 1)
        put(received[1], 0)

    @pl.when(jnp.logical_not(even("map")))
    def _():
        put(received[0], 0)
        put(received[1], 1)


def half_step(kind, n_depth, last, refs):
    layers, columns = refs[0].shape[1:3]
    if kind == "speed":
        speed, stress, dtb, lift_in = refs[:4]
        moving, n = stress, 4
        map_spec, depth_spec, out_map, out_depth = STRESS_MAP, STRESS_DEPTH, SPEED_MAP, SPEED_DEPTH
    else:
        stress, speed, dtl, dts = refs[:4]
        moving, n = speed, 4
        map_spec, depth_spec, out_map, out_depth = SPEED_MAP, SPEED_DEPTH, STRESS_MAP, STRESS_DEPTH
    recv_depth, recv_map = refs[n : n + n_depth], refs[n + n_depth : n + n_depth + 2]
    outs = refs[n + n_depth + 2 :]
    below, above, wide = outs[-3:]
    new = outs[0]
    outs = outs[1:-3]
    if kind == "speed":
        lift_out, outs = outs[0], outs[1:]
    take_halos(depth_spec, "depth", recv_depth, below, above)
    build_map(map_spec, moving, wide, recv_map, layers, columns)
    low, high = slots(depth_spec, 0), slots(depth_spec, 1)

    def layer(p):
        def z(field):
            def at(offset):
                if isinstance(p, int) and p + offset < 0:
                    return below[low[(field, p + offset)]]
                if isinstance(p, int) and p + offset >= layers:
                    return above[high[(field, p + offset - layers)]]
                return moving[field, p + offset]

            return at

        def x(field):
            return lambda offset: wide[field, p, pl.ds(PAD + offset, columns)]

        if kind == "speed":
            b = dtb[p]
            new[0, p] = speed[0, p] + b * (
                diff_forward(x(0)) + backward_y(stress[1, p]) + diff_backward(z(2))
            )
            new[1, p] = speed[1, p] + b * (
                diff_backward(x(1)) + forward_y(stress[5, p]) + diff_backward(z(3))
            )
            vz = speed[2, p] + b * (
                diff_backward(x(2)) + backward_y(stress[3, p]) + diff_forward(z(4))
            )
            new[2, p] = vz
            if isinstance(p, int) and p == 0:
                lift_out[0] = lift_in[...] + time_step * vz
                lift_out[1] = vz
        else:
            l, s = dtl[p], dts[p]
            vx, vy, vz = speed[0, p], speed[1, p], speed[2, p]
            ex, ey, ez = diff_backward(x(0)), backward_y(vy), diff_backward(z(2))
            spread = l * (ex + ey + ez)
            s2 = 2.0 * s
            new[0, p] = stress[0, p] + (spread + s2 * ex)
            new[4, p] = stress[4, p] + (spread + s2 * ez)
            new[5, p] = stress[5, p] + (spread + s2 * ey)
            new[1, p] = stress[1, p] + s * (forward_y(vx) + diff_forward(x(1)))
            new[2, p] = stress[2, p] + s * (diff_forward(z(0)) + diff_forward(x(2)))
            new[3, p] = stress[3, p] + s * (diff_forward(z(1)) + forward_y(vz))

    for p in (0, 1, layers - 2, layers - 1):
        layer(p)

    def body(p, _):
        layer(p)
        return 0

    lax.fori_loop(2, layers - 2, body, 0)
    if not last:

        def read(field, at_layer, at_column):
            if at_column is None:
                return new[field, at_layer]
            return new[field, :, at_column]

        emit_all(out_map, out_depth, read, layers, columns, outs[:n_depth], outs[n_depth : n_depth + 2])
        if kind == "speed":

            @pl.when(even("depth"))
            def _():
                outs[0][pl.ds(SLOTS, 2)] = lift_out[...]


def params(**kw):
    return pltpu.CompilerParams(vmem_limit_bytes=24 << 20, **kw)


def run_half(kind, args, recv_depth, recv_map, last=False):
    layers, columns = args[0].shape[1:3]
    n_depth = len(recv_depth)
    plane = (columns, LANES)
    out = [jax.ShapeDtypeStruct(args[0].shape, F32)]
    if kind == "speed":
        out.append(jax.ShapeDtypeStruct((2,) + plane, F32))
    if not last:
        extra = 2 if kind == "speed" else 0
        out += [jax.ShapeDtypeStruct((SLOTS + extra,) + plane, F32)] * n_depth
        out += [jax.ShapeDtypeStruct((SLOTS, layers, LANES), F32)] * 2

    def kernel(*refs):
        half_step(kind, n_depth, last, refs)

    ins = list(args) + list(recv_depth) + list(recv_map)
    return pl.pallas_call(
        kernel,
        out_shape=out,
        in_specs=[VMEM] * len(ins),
        out_specs=[VMEM] * len(out),
        scratch_shapes=[
            pltpu.VMEM((SLOTS,) + plane, F32),
            pltpu.VMEM((SLOTS,) + plane, F32),
            pltpu.VMEM((3, layers, columns + 2 * PAD, LANES), F32),
        ],
        compiler_params=params(),
        name=kind,
    )(*ins)


def exchange(sends, n_depth):
    depth = [swap(sends[i], "depth", i) for i in range(n_depth)]
    return depth, [swap(sends[n_depth + i], "map", i) for i in range(2)]


OCEAN = ("height", "wet", "index", "flux_x", "flux_y", "depth_x", "depth_y")


def ocean_prep_kernel(n_depth, *refs):
    n = len(OCEAN)
    own, recv = refs[:n], refs[n : n + n_depth]
    wides = refs[n + n_depth : 2 * n + n_depth]
    to_west, to_east = refs[2 * n + n_depth :]
    rows, cols = own[0].shape
    tiles = cols // LANES
    lane = lax.broadcasted_iota(jnp.int32, (rows + 2 * PAD, LANES), 1)
    west = jnp.zeros((rows + 2 * PAD, LANES), F32)
    east = west

    def lines(ref, i, k, t):
        return ref[SLOTS, pl.ds((i * 2 + k) * tiles + t, 1), :]

    for i in range(n):
        wide = wides[i]
        wide[pl.ds(0, PAD)] = jnp.zeros((PAD, cols), F32)
        wide[pl.ds(PAD + rows, PAD)] = jnp.zeros((PAD, cols), F32)
        wide[pl.ds(PAD, rows)] = own[i][...].astype(F32)

        def put(ref, side):
            for k in range(2):
                at = PAD - 2 + k if side == 0 else PAD + rows + k
                for t in range(tiles):
                    wide[pl.ds(at, 1), pl.ds(t * LANES, LANES)] = lines(ref, i, k, t)

        @pl.when(even("depth"))
        def _():
            put(recv[0], 1)
            if n_depth > 1:
                put(recv[1], 0)

        @pl.when(jnp.logical_not(even("depth")))
        def _():
            put(recv[0], 0)
            if n_depth > 1:
                put(recv[1], 1)

        here = jnp.logical_or(lane == 2 * i, lane == 2 * i + 1)
        west = jnp.where(here, roll(wide[:, pl.ds(0, LANES)], 2 * i), west)
        east = jnp.where(here, roll(wide[:, pl.ds(cols - LANES, LANES)], 2 * i + 2), east)
    to_west[...] = west
    to_east[...] = east


def ocean_pick_kernel(own_table, far_table, index, height, wet, west, east, level, source, first, second):
    rows, cols = index.shape
    crust = own_table.shape[1]
    tiles = cols // LANES

    def pick(table):
        def body(i, _):
            at = pl.multiple_of(i * 8, 8)
            for t in range(tiles):
                here = (pl.ds(at, 8), pl.ds(t * LANES, LANES))
                cell = index[here].astype(jnp.int32)
                upper, lower = cell // LANES, lax.rem(cell, LANES)
                a = jnp.zeros((8, LANES), F32)
                b = jnp.zeros((8, LANES), F32)
                for row in range(crust):
                    chosen = upper == row
                    la = jnp.broadcast_to(table(0, row), (8, LANES))
                    lb = jnp.broadcast_to(table(1, row), (8, LANES))
                    a = jnp.where(chosen, jnp.take_along_axis(la, lower, axis=1), a)
                    b = jnp.where(chosen, jnp.take_along_axis(lb, lower, axis=1), b)
                w = wet[here]
                level[here] = w * (height[here] + a)
                source[here] = w * b
            return 0

        lax.fori_loop(0, rows // 8, body, 0)

    @pl.when(lax.axis_index("depth") == 0)
    def _():
        pick(lambda k, row: own_table[k, pl.ds(row, 1)])

    @pl.when(lax.axis_index("depth") != 0)
    def _():
        pick(lambda k, row: far_table[far_table.shape[0] - 2 + k, pl.ds(row, 1)])

    lane = lax.broadcasted_iota(jnp.int32, (rows, LANES), 1)

    def packed(static, start, shift):
        out = static[...]
        for i, ref in ((0, level), (2, source)):
            here = jnp.logical_or(lane == 2 * i, lane == 2 * i + 1)
            out = jnp.where(here, roll(ref[:, pl.ds(start, LANES)], 2 * i + shift), out)
        return out

    to_west = packed(west, 0, 0)
    to_east = packed(east, cols - LANES, 2)

    @pl.when(even("map"))
    def _():
        first[...] = to_east
        second[...] = to_west

    @pl.when(jnp.logical_not(even("map")))
    def _():
        first[...] = to_west
        second[...] = to_east


def ocean_kernel(*refs):
    n = len(OCEAN)
    wides, (first, second) = refs[:n], refs[n : n + 2]
    height_out, flux_out = refs[n + 2 : n + 4]
    full = refs[n + 4]
    height, cols = wides[0].shape
    rows = height - 2 * PAD
    lane = lax.broadcasted_iota(jnp.int32, (height, LANES), 1)

    def fill(east, west):
        e, w = east[...], west[...]
        for i in range(n):
            full[i, :, pl.ds(0, cols)] = wides[i][...]
            beside = jnp.where(lane < 2, roll(e, -2 * i), 0.0)
            full[i, :, pl.ds(cols, LANES)] = jnp.where(lane >= LANES - 2, roll(w, -2 - 2 * i), beside)

    @pl.when(even("map"))
    def _():
        fill(first, second)

    @pl.when(jnp.logical_not(even("map")))
    def _():
        fill(second, first)

    def row_roll(x, by):
        return pltpu.roll(x, by % height, 0)

    level, wet, source, flux_x, flux_y, depth_x, depth_y = (full[i] for i in range(n))
    mask_x = wet * roll(wet, -1)
    mask_y = wet * row_roll(wet, -1)
    depth_x, depth_y = depth_x * mask_x, depth_y * mask_y
    flux_x, flux_y = flux_x * mask_x, flux_y * mask_y
    for _ in range(OSTEPS):
        flux_x = flux_x - ocean_step * gravity * depth_x * (roll(level, -1) - level)
        flux_y = flux_y - ocean_step * gravity * depth_y * (row_roll(level, -1) - level)
        level = (
            level
            - ocean_step * wet * ((flux_x - roll(flux_x, 1)) + (flux_y - row_roll(flux_y, 1)))
            + ocean_step * source
        )
    own = slice(PAD, PAD + rows)
    height_out[...] = level[own, :cols]
    flux_out[0] = flux_x[own, :cols]
    flux_out[1] = flux_y[own, :cols]


def call(kernel, out, ins, name, in_specs=None, scratch=()):
    return pl.pallas_call(
        kernel,
        out_shape=out,
        in_specs=in_specs or [VMEM] * len(ins),
        out_specs=[VMEM] * len(out),
        scratch_shapes=list(scratch),
        compiler_params=params(),
        name=name,
    )(*ins)


def per_device(
    velocity,
    stress,
    region,
    lame_table,
    shear_table,
    buoyancy_table,
    height,
    discharge,
    face_depth,
    wet,
    seafloor_index,
):
    layers, columns = region.shape[:2]
    rows, cols = height.shape
    n_depth = min(2, lax.axis_size("depth") - 1)
    shape = jax.ShapeDtypeStruct
    plane = (columns, LANES)
    ocean = [
        height,
        wet.astype(F32),
        seafloor_index.astype(F32),
        discharge[0],
        discharge[1],
        face_depth[0],
        face_depth[1],
    ]
    n = len(ocean)
    sends = call(
        functools.partial(edge_kernel, n_depth, n, layers, columns),
        [shape((SLOTS + 1,) + plane, F32)] * n_depth + [shape((SLOTS, layers, LANES), F32)] * 2,
        [stress] + ocean,
        "edges",
        in_specs=[ANY] * (1 + n),
        scratch=[
            pltpu.VMEM((3, layers, PAD, LANES), F32),
            pltpu.VMEM((3, layers, PAD, LANES), F32),
            pltpu.VMEM((3, 2) + plane, F32),
            pltpu.VMEM((3, 2) + plane, F32),
            pltpu.VMEM((n, PAD, cols), F32),
            pltpu.VMEM((n, PAD, cols), F32),
            pltpu.SemaphoreType.DMA((4 + 2 * n,)),
        ],
    )
    recv = exchange(sends, n_depth)
    dtb, dtl, dts = call(
        material_kernel,
        [shape(region.shape, F32)] * 3,
        [lame_table, shear_table, buoyancy_table, region],
        "material",
        in_specs=[SMEM] * 3 + [VMEM],
    )
    tall = (rows + 2 * PAD, cols)
    *wides, west, east = call(
        functools.partial(ocean_prep_kernel, n_depth),
        [shape(tall, F32)] * n + [shape((tall[0], LANES), F32)] * 2,
        ocean + recv[0],
        "ocean_prep",
    )
    speeds, forces, lift = velocity, stress, jnp.zeros(plane, F32)
    for turn in range(ITERS):
        speeds, table, *sends = run_half("speed", (speeds, forces, dtb, lift), *recv)
        lift = table[0]
        recv = exchange(sends, n_depth)
        last = turn == ITERS - 1
        forces, *sends = run_half("stress", (forces, speeds, dtl, dts), *recv, last=last)
        if not last:
            recv = exchange(sends, n_depth)
    if n_depth > 1:
        mine = lax.axis_index("depth") == 0
        table = lax.psum(jnp.where(mine, table, jnp.zeros_like(table)), "depth")
        far = table
    else:
        far = recv[0][0]
    level, source, first, second = call(
        ocean_pick_kernel,
        [shape(tall, F32)] * 2 + [shape((tall[0], LANES), F32)] * 2,
        [table, far, wides[2], wides[0], wides[1], west, east],
        "ocean_pick",
    )
    first, second = swap(first, "map", 0), swap(second, "map", 1)
    level_out, flux_out = call(
        ocean_kernel,
        [shape((rows, cols), F32), shape((2, rows, cols), F32)],
        [level, wides[1], source] + list(wides[3:]) + [first, second],
        "ocean",
        scratch=[pltpu.VMEM((n, tall[0], cols + LANES), F32)],
    )
    return (speeds, forces, level_out, flux_out)


def solution(mesh):
    return jax.shard_map(
        per_device,
        mesh=mesh,
        in_specs=(
            P(None, "depth", "map", None),
            P(None, "depth", "map", None),
            P("depth", "map", None),
            P(),
            P(),
            P(),
            P("depth", "map"),
            P(None, "depth", "map"),
            P(None, "depth", "map"),
            P("depth", "map"),
            P("depth", "map"),
        ),
        out_specs=(
            P(None, "depth", "map", None),
            P(None, "depth", "map", None),
            P("depth", "map"),
            P(None, "depth", "map"),
        ),
        check_vma=False,
    )
```
